512 devices in a mesh: seg: 32 (over z_lo, y), blk: 16 (over z_hi, x, core).
Axes of the slice: x: 4, y: 4, z: 16 (z_hi: 2, z_lo: 8; z = z_hi * 8 + z_lo), core: 2. Of those that a mesh axis runs over, the one named last changes fastest.
Arguments:
- queries: float32 [65536, 1024], P(('seg', 'blk')), may hold values from -5 to 5
- keys: float32 [65536, 256], P(('seg', 'blk')), may hold values from -5 to 5
- values: float32 [65536, 256], P(('seg', 'blk')), may hold values from -6 to 6
- gate_logit: float32 [8], replicated, may hold values from -3 to 3
- memory_gain: float32 [1024], replicated, may hold values from 0.5 to 2
Outputs:
- mixed: float32 [65536, 1024], P(('seg', 'blk'))
The draws below stay inside these ranges and needn't reach their ends.
All inputs are finite; a program needn't handle non-finite values.
Results may differ from the reference program's by a relative error of at most 0.0003.
Values sent between devices are 32-bit elements; how exact they have to be, the bound alone decides.
A program may use at most 64 MiB of HBM per device.

```python
import math
import jax
import jax.numpy as jnp
from jax import lax

ROWS = 128
QH = 8
KVH = 2
GROUP = 4
HD = 128
SEQ = 65536
N_SEG = 32
N_BLK = 16


def draw_keys(key, part):
    base = jnp.clip(jax.random.normal(jax.random.fold_in(key, 11), (SEQ, KVH * HD), jnp.float32), -5.0, 5.0)
    return base


def draw_queries(key, part):
    base = jnp.clip(jax.random.normal(jax.random.fold_in(key, 13), (SEQ, QH * HD), jnp.float32), -5.0, 5.0)
    return base


def block_scale(own_key, shape, cuts, low, largest):
    level, own = 1.0, jax.random.fold_in(own_key, 6)
    for dim, shards_of in cuts:
        draws = jnp.exp(jax.random.uniform(jax.random.fold_in(own, dim), (shards_of,), jnp.float32, low / len(cuts), largest / len(cuts)))
        level = level * jnp.repeat(draws, shape[dim] // shards_of).reshape([-1 if axis == dim else 1 for axis in range(len(shape))])
    return level


def gaussian(key, extent, deviation, bound, shards=(), kind=jnp.bfloat16):
    level = block_scale(key, extent, shards, -0.22, 0.18) if shards else 1.0
    array = jax.random.normal(key, extent, jnp.float32) * deviation * level
    return jnp.minimum(jnp.maximum(array, -bound), bound).astype(kind)


def setup_inputs(seed: int = 0) -> dict:
    splits = jax.random.split(jax.random.key(seed), 6)
    queries = draw_queries(jax.random.fold_in(splits[5], 71), 0)
    keys = draw_keys(jax.random.fold_in(splits[5], 71), 0)
    values = gaussian(splits[2], (SEQ, KVH * HD), 1.0, 6.0, ((0, 512),), jnp.float32)
    gate_logit = jnp.clip(jax.random.uniform(splits[3], (QH,), jnp.float32, -3.0, 3.0), -3.0, 3.0)
    memory_gain = jnp.clip(jnp.exp(jax.random.uniform(splits[4], (QH * HD,), jnp.float32, math.log(0.5), math.log(2.0))), 0.5, 2.0)
    return dict(queries=queries, keys=keys, values=values, gate_logit=gate_logit, memory_gain=memory_gain)


HIGH = lax.Precision.HIGHEST

def sigma_map(x):
    return jnp.where(x > 0, x + 1.0, jnp.exp(jnp.minimum(x, 0.0)))

def segment_out(operands):
    q_seg, k_seg, v_seg, memory_seg = operands
    length = q_seg.shape[0]
    q_heads = q_seg.reshape(length, KVH, GROUP, HD)
    k_heads = k_seg.reshape(length, KVH, HD)
    v_heads = v_seg.reshape(length, KVH, HD)
    qpos = jnp.arange(length, dtype=jnp.int32)
    causal = qpos[None, :] <= qpos[:, None]

    def one_head(inputs):
        qh, kh, vh = inputs
        scores = jnp.einsum('rgd,nd->grn', qh, kh, precision=HIGH) / jnp.sqrt(jnp.float32(HD))
        scores = jnp.where(causal[None], scores, -1e+30)
        top = lax.optimization_barrier(jnp.max(scores, axis=-1, keepdims=True))
        weights = jnp.where(causal[None], jnp.exp(scores - top), 0.0)
        total = lax.optimization_barrier(jnp.sum(weights, axis=-1, keepdims=True))
        return jnp.einsum('grn,nd->grd', weights, vh, precision=HIGH) / total
    attention = lax.map(one_head, (jnp.transpose(q_heads, (1, 0, 2, 3)), jnp.transpose(k_heads, (1, 0, 2)), jnp.transpose(v_heads, (1, 0, 2))))
    retrieval = jnp.einsum('rkgd,kde->kgre', sigma_map(q_heads), memory_seg, precision=HIGH)
    return (attention, retrieval)

def reference(queries, keys, values, gate_logit, memory_gain):
    seg_count = N_SEG
    length = ROWS * N_BLK
    k_all = keys.reshape(seg_count, length, KVH, HD)
    v_all = values.reshape(seg_count, length, KVH, HD)
    partial_value = jnp.einsum('gskd,gske->gkde', sigma_map(k_all), v_all, precision=HIGH)
    memory = jnp.cumsum(partial_value, axis=0) - partial_value
    attention, retrieval = lax.map(segment_out, (queries.reshape(seg_count, length, QH * HD), keys.reshape(seg_count, length, KVH * HD), values.reshape(seg_count, length, KVH * HD), memory))
    rms = jnp.sqrt(lax.optimization_barrier(jnp.mean(retrieval * retrieval, axis=-1, keepdims=True)) + 1e-06)
    gain = memory_gain.reshape(KVH, GROUP, 1, HD)
    normed = retrieval / rms * gain
    gate = jax.nn.sigmoid(gate_logit).reshape(KVH, GROUP, 1, 1)
    mixed = gate * normed + (1.0 - gate) * attention
    return jnp.transpose(mixed, (0, 3, 1, 2, 4)).reshape(seg_count * length, QH * HD)
```

```python
import jax
import jax.numpy as jnp
from jax import lax
from jax.experimental import pallas as pl
from jax.experimental.pallas import tpu as pltpu
from jax.sharding import PartitionSpec as P

KVH = 2
GROUP = 4
HD = 128
NX = 4
NY = 4
NZ = 8
NCH = 4
LOG2E = 1.4426950408889634
MASKED = -1e30
MESH = pl.DeviceIdType.MESH
HIGH = lax.Precision.HIGHEST
NT = (((1,), (1,)), ((), ()))
TN = (((0,), (0,)), ((), ()))
NN = (((1,), (0,)), ((), ()))


def sigma_map(x):
    return jnp.where(x > 0, x + 1.0, jnp.exp(jnp.minimum(x, 0.0)))


def halves(x):
    top = x.astype(jnp.bfloat16)
    return top, (x - top.astype(jnp.float32)).astype(jnp.bfloat16)


def mm(a, b, dims):
    return lax.dot_general(a, b, dims, preferred_element_type=jnp.float32)


def kernel(
    q_hbm,
    k_hbm,
    v_hbm,
    gate_ref,
    gain_ref,
    o_ref,
    q_ref,
    kv_ref,
    qs_ref,
    m_ref,
    l_ref,
    acc_ref,
    partial_ref,
    parts_ref,
    shard_ref,
    ypart_ref,
    total_ref,
    zpart_ref,
    other_ref,
    stage_ref,
    own_ref,
    memory_ref,
    load_sem,
    zs,
    zr,
    xs,
    xr,
    ss,
    sr,
    ps,
    pr,
    ys,
    yr,
    ts,
    tr,
    fs,
    fr,
    ms,
    mr,
    gs,
    gr,
):
    seg = lax.axis_index("seg")
    blk = lax.axis_index("blk")
    z_lo = lax.div(seg, NY)
    y = lax.rem(seg, NY)
    z_hi = lax.div(blk, 2 * NX)
    j = lax.rem(blk, 2 * NX)
    x = lax.div(j, 2)
    c = lax.rem(j, 2)
    rows = q_ref.shape[0]
    step = rows // NCH

    def at(zh, zl, xx, yy, cc):
        return {"seg": zl * NY + yy, "blk": zh * 2 * NX + xx * 2 + cc}

    def near(dx, dc):
        return at(z_hi, z_lo, lax.rem(x + dx, NX), y, lax.rem(c + dc, 2))

    def along_y(dy):
        return at(z_hi, z_lo, x, lax.rem(y + dy, NY), c)

    def remote(src, dst, send, recv, device):
        return pltpu.make_async_remote_copy(
            src_ref=src,
            dst_ref=dst,
            send_sem=send,
            recv_sem=recv,
            device_id=device,
            device_id_type=MESH,
        )

    others = [(dx, dc) for dx in range(NX) for dc in range(2) if (dx, dc) != (0, 0)]

    loads = [
        pltpu.make_async_copy(
            hbm.at[pl.ds(ch * step, step)], kv_ref.at[0, ch, c, x, kv], load_sem.at[kv, ch]
        )
        for ch in range(NCH)
        for kv, hbm in enumerate((k_hbm, v_hbm))
    ]
    q_load = pltpu.make_async_copy(q_hbm, q_ref, load_sem.at[2, 0])
    for load in loads:
        load.start()
    q_load.start()
    zpart_ref[...] = jnp.zeros_like(zpart_ref)

    barrier = pltpu.get_barrier_semaphore()
    opposite = at(1 - z_hi, z_lo, x, y, c)
    greeted = [near(dx, dc) for dx, dc in others]
    greeted += [along_y(dy) for dy in range(1, NY)]
    greeted += [opposite]
    for d in range(1, NZ):
        for e in range(2):
            greeted.append(at(lax.rem(z_hi + e, 2), lax.rem(z_lo + d, NZ), x, y, c))
    for device in greeted:
        pl.semaphore_signal(barrier, inc=1, device_id=device, device_id_type=MESH)

    for load in loads:
        load.wait()
    for k in range(KVH):
        cols = pl.ds(k * HD, HD)
        key = kv_ref[0, :, c, x, 0, :, cols].reshape(rows, HD)
        value = kv_ref[0, :, c, x, 1, :, cols].reshape(rows, HD)
        partial_ref[pl.ds(k * 4, 4)] = lax.dot_general(
            sigma_map(key), value, TN, precision=HIGH, preferred_element_type=jnp.float32
        ).reshape(4, 32, HD)
    q_load.wait()
    scale = LOG2E / (HD**0.5)
    for k in range(KVH):
        for g in range(GROUP):
            h = k * GROUP + g
            top, low = halves(q_ref[:, pl.ds(h * HD, HD)] * scale)
            qs_ref[k, pl.ds(g * rows, rows), pl.ds(0, HD)] = top
            qs_ref[k, pl.ds(g * rows, rows), pl.ds(HD, HD)] = low
    m_ref[...] = jnp.full_like(m_ref, MASKED)
    l_ref[...] = jnp.zeros_like(l_ref)
    acc_ref[...] = jnp.zeros_like(acc_ref)

    pl.semaphore_wait(barrier, len(greeted))

    def across(ch):
        return remote(
            kv_ref.at[0, ch, c, x], kv_ref.at[1, ch, c, x], zs.at[ch], zr.at[ch], opposite
        )

    def spread(half, ch, dx):
        item = kv_ref.at[half, ch, c, x]
        return remote(
            item, item, xs.at[half, ch, dx - 1], xr.at[half, ch, dx - 1], near(dx, 0)
        )

    def share(half, ch, dx):
        item = kv_ref.at[half, ch, c, lax.rem(x + NX - dx, NX)]
        return remote(item, item, ss.at[half, ch, dx], sr.at[half, ch, dx], near(0, 1))

    @pl.when(z_hi == 0)
    def _():
        for ch in range(NCH):
            across(ch).start()

    def scatter(n):
        dx, dc = others[n]
        target = lax.rem(x + dx, NX) * 2 + lax.rem(c + dc, 2)
        return remote(
            partial_ref.at[target], parts_ref.at[j], ps.at[n], pr.at[n], near(dx, dc)
        )

    for n in range(len(others)):
        scatter(n).start()
    parts_ref[j] = partial_ref[j]

    def begin(half, ch):
        for dx in range(1, NX):
            spread(half, ch, dx).start()
        share(half, ch, 0).start()

    def pass_on(half, ch):
        for dx in range(1, NX):
            spread(half, ch, dx).wait_recv()
            share(half, ch, dx).start()

    def arrive(half, ch):
        for dx in range(NX):
            share(half, ch, dx).wait_recv()

    @pl.loop(0, NCH)
    def _(ch):
        begin(0, ch)

    for n in range(len(others)):
        scatter(n).wait_recv()
    shard_ref[...] = jnp.sum(parts_ref[...], axis=0).reshape(NY, 8, HD)

    def turn(dy):
        return remote(
            shard_ref.at[lax.rem(y + dy, NY)],
            ypart_ref.at[y],
            ys.at[dy - 1],
            yr.at[dy - 1],
            along_y(dy),
        )

    for dy in range(1, NY):
        turn(dy).start()
    ypart_ref[y] = shard_ref[y]

    @pl.loop(0, NCH)
    def _(ch):
        pass_on(0, ch)

    for dy in range(1, NY):
        turn(dy).wait_recv()
    total_ref[...] = jnp.sum(ypart_ref[...], axis=0)

    def onward(d, e):
        return remote(
            total_ref,
            zpart_ref.at[d - 1, e],
            ts.at[d - 1, e],
            tr.at[d - 1, e],
            at(lax.rem(z_hi + e, 2), lax.rem(z_lo + d, NZ), x, y, c),
        )

    over = remote(ypart_ref, other_ref, fs, fr, opposite)
    over.start()
    for d in range(1, NZ):

        @pl.when(z_lo + d < NZ)
        def _(d=d):
            for e in range(2):
                onward(d, e).start()

    qpos = j * rows + lax.rem(
        lax.broadcasted_iota(jnp.int32, (GROUP * rows, 2 * HD), 0), rows
    )
    slot = lax.broadcasted_iota(jnp.int32, (GROUP * rows, 2 * HD), 1)
    per = NX * step
    base_kpos = (
        lax.rem(lax.div(slot, step), NX) * 2 + lax.div(slot, per)
    ) * rows + lax.rem(slot, step)

    def attend(half, ch):
        for k in range(KVH):
            cols = pl.ds(k * HD, HD)
            key = kv_ref[half, ch, :, :, 0, :, cols].reshape(2 * NX * step, HD)
            value = kv_ref[half, ch, :, :, 1, :, cols].reshape(2 * NX * step, HD)
            k_top, k_low = halves(key)
            v_both = jnp.concatenate(halves(value), axis=1)
            q_both = qs_ref[k]
            scores = mm(q_both, jnp.concatenate((k_top, k_top), axis=1), NT)
            scores += mm(qs_ref[k, :, pl.ds(0, HD)], k_low, NT)
            if half == 0:
                scores = jnp.where(base_kpos + ch * step <= qpos, scores, MASKED)
            old = m_ref[k]
            new = jnp.maximum(old, jnp.max(scores, axis=1, keepdims=True))
            m_ref[k] = new
            decay = jnp.exp2(old - new)
            weights = jnp.exp2(scores - jnp.concatenate((new, new), axis=1))
            l_ref[k] = l_ref[k] * decay + weights[:, :HD] + weights[:, HD:]
            w_top, w_low = halves(weights)
            both = mm(w_top, v_both, NN) + mm(w_low, v_both, NN)
            acc_ref[k] = acc_ref[k] * decay + both[:, :HD] + both[:, HD:]

    @pl.loop(0, NCH)
    def _(ch):
        arrive(0, ch)
        attend(0, ch)

    for d in range(1, NZ):

        @pl.when(z_lo >= d)
        def _(d=d):
            for e in range(2):
                onward(d, e).wait_recv()

    over.wait_recv()
    carried = jnp.sum(zpart_ref[...], axis=(0, 1))
    for row in range(NY):
        stage_ref[row] = carried
        carried = carried + ypart_ref[row] + other_ref[row]

    def back(dy):
        return remote(
            stage_ref.at[lax.rem(y + dy, NY)],
            own_ref.at[y],
            ms.at[dy - 1],
            mr.at[dy - 1],
            along_y(dy),
        )

    for dy in range(1, NY):
        back(dy).start()
    own_ref[y] = stage_ref[y]
    for dy in range(1, NY):
        back(dy).wait_recv()

    def gather(n):
        dx, dc = others[n]
        return remote(own_ref, memory_ref.at[j], gs.at[n], gr.at[n], near(dx, dc))

    for n in range(len(others)):
        gather(n).start()
    memory_ref[j] = own_ref[...]
    for n in range(len(others)):
        gather(n).wait_recv()

    gates = 1.0 / (1.0 + jnp.exp(-gate_ref[...]))
    for k in range(KVH):
        memory = memory_ref[pl.ds(k * 4, 4)].reshape(HD, HD)
        for g in range(GROUP):
            h = k * GROUP + g
            cols = pl.ds(h * HD, HD)
            got = lax.dot_general(
                sigma_map(q_ref[:, cols]),
                memory,
                NN,
                precision=HIGH,
                preferred_element_type=jnp.float32,
            )
            rms = jnp.sqrt(jnp.mean(got * got, axis=1, keepdims=True) + 1e-6)
            gate = gates[:, h : h + 1]
            o_ref[:, cols] = (got / rms) * (gain_ref[h : h + 1, :] * gate)

    @pl.when(z_hi == 1)
    def _():
        @pl.loop(0, NCH)
        def _(ch):
            across(ch).wait_recv()
            begin(1, ch)
            pass_on(1, ch)
            arrive(1, ch)
            attend(1, ch)

        @pl.loop(0, NCH)
        def _(ch):
            for dx in range(1, NX):
                spread(1, ch, dx).wait_send()
            for dx in range(NX):
                share(1, ch, dx).wait_send()

    for k in range(KVH):
        for g in range(GROUP):
            h = k * GROUP + g
            cols = pl.ds(h * HD, HD)
            part = pl.ds(g * rows, rows)
            total = jnp.sum(l_ref[k, part], axis=1, keepdims=True)
            gate = gates[:, h : h + 1]
            o_ref[:, cols] += acc_ref[k, part] * ((1.0 - gate) / total)

    @pl.when(z_hi == 0)
    def _():
        for ch in range(NCH):
            across(ch).wait_send()

    @pl.loop(0, NCH)
    def _(ch):
        for dx in range(1, NX):
            spread(0, ch, dx).wait_send()
        for dx in range(NX):
            share(0, ch, dx).wait_send()

    for n in range(len(others)):
        scatter(n).wait_send()
        gather(n).wait_send()
    for dy in range(1, NY):
        turn(dy).wait_send()
        back(dy).wait_send()
    over.wait_send()
    for d in range(1, NZ):

        @pl.when(z_lo + d < NZ)
        def _(d=d):
            for e in range(2):
                onward(d, e).wait_send()


def on_device(queries, keys, values, gate_logit, memory_gain):
    rows = queries.shape[0]
    heads = KVH * GROUP
    f32 = jnp.float32
    sem = pltpu.SemaphoreType.DMA
    peers = 2 * NX - 1
    return pl.pallas_call(
        kernel,
        out_shape=jax.ShapeDtypeStruct((rows, heads * HD), f32),
        in_specs=[pl.BlockSpec(memory_space=pl.ANY)] * 3
        + [pl.BlockSpec(memory_space=pltpu.VMEM)] * 2,
        out_specs=pl.BlockSpec(memory_space=pltpu.VMEM),
        scratch_shapes=[
            pltpu.VMEM((rows, heads * HD), f32),
            pltpu.VMEM((2, NCH, 2, NX, 2, rows // NCH, KVH * HD), f32),
            pltpu.VMEM((KVH, GROUP * rows, 2 * HD), jnp.bfloat16),
            pltpu.VMEM((KVH, GROUP * rows, HD), f32),
            pltpu.VMEM((KVH, GROUP * rows, HD), f32),
            pltpu.VMEM((KVH, GROUP * rows, HD), f32),
            pltpu.VMEM((2 * NX, 32, HD), f32),
            pltpu.VMEM((2 * NX, 32, HD), f32),
            pltpu.VMEM((NY, 8, HD), f32),
            pltpu.VMEM((NY, 8, HD), f32),
            pltpu.VMEM((8, HD), f32),
            pltpu.VMEM((NZ - 1, 2, 8, HD), f32),
            pltpu.VMEM((NY, 8, HD), f32),
            pltpu.VMEM((NY, 8, HD), f32),
            pltpu.VMEM((NY, 8, HD), f32),
            pltpu.VMEM((2 * NX, NY, 8, HD), f32),
            sem((3, NCH)),
            sem((NCH,)),
            sem((NCH,)),
            sem((2, NCH, NX - 1)),
            sem((2, NCH, NX - 1)),
            sem((2, NCH, NX)),
            sem((2, NCH, NX)),
            sem((peers,)),
            sem((peers,)),
            sem((NY - 1,)),
            sem((NY - 1,)),
            sem((NZ - 1, 2)),
            sem((NZ - 1, 2)),
            sem,
            sem,
            sem((NY - 1,)),
            sem((NY - 1,)),
            sem((peers,)),
            sem((peers,)),
        ],
        compiler_params=pltpu.CompilerParams(collective_id=0, has_side_effects=True),
    )(
        queries,
        keys,
        values,
        gate_logit.reshape(1, heads),
        memory_gain.reshape(heads, HD),
    )


def solution(mesh):
    return jax.shard_map(
        on_device,
        mesh=mesh,
        in_specs=(
            P(("seg", "blk"), None),
            P(("seg", "blk"), None),
            P(("seg", "blk"), None),
            P(),
            P(),
        ),
        out_specs=P(("seg", "blk"), None),
        check_vma=False,
    )
```

```python
import jax
import jax.numpy as jnp
from jax import lax
from jax.experimental import pallas as pl
from jax.experimental.pallas import tpu as pltpu
from jax.sharding import PartitionSpec as P

KVH = 2
GROUP = 4
HD = 128
NX = 4
NY = 4
NZ = 8
NCH = 4
LOG2E = 1.4426950408889634
MASKED = -1e30
MESH = pl.DeviceIdType.MESH
HIGH = lax.Precision.HIGHEST
NT = (((1,), (1,)), ((), ()))
TN = (((0,), (0,)), ((), ()))
NN = (((1,), (0,)), ((), ()))


def sigma_map(x):
    return jnp.where(x > 0, x + 1.0, jnp.exp(jnp.minimum(x, 0.0)))


def halves(x):
    top = x.astype(jnp.bfloat16)
    return top, (x - top.astype(jnp.float32)).astype(jnp.bfloat16)


def mm(a, b, dims):
    return lax.dot_general(a, b, dims, preferred_element_type=jnp.float32)


def kernel(
    q_hbm,
    k_hbm,
    v_hbm,
    gate_ref,
    gain_ref,
    o_ref,
    q_ref,
    kv_ref,
    qs_ref,
    m_ref,
    l_ref,
    acc_ref,
    partial_ref,
    parts_ref,
    shard_ref,
    ypart_ref,
    total_ref,
    zpart_ref,
    other_ref,
    stage_ref,
    own_ref,
    memory_ref,
    load_sem,
    zs,
    zr,
    xs,
    xr,
    ss,
    sr,
    ps,
    pr,
    ys,
    yr,
    ts,
    tr,
    fs,
    fr,
    ms,
    mr,
    gs,
    gr,
):
    seg = lax.axis_index("seg")
    blk = lax.axis_index("blk")
    z_lo = lax.div(seg, NY)
    y = lax.rem(seg, NY)
    z_hi = lax.div(blk, 2 * NX)
    j = lax.rem(blk, 2 * NX)
    x = lax.div(j, 2)
    c = lax.rem(j, 2)
    rows = q_ref.shape[0]
    step = rows // NCH

    def at(zh, zl, xx, yy, cc):
        return {"seg": zl * NY + yy, "blk": zh * 2 * NX + xx * 2 + cc}

    def near(dx, dc):
        return at(z_hi, z_lo, lax.rem(x + dx, NX), y, lax.rem(c + dc, 2))

    def along_y(dy):
        return at(z_hi, z_lo, x, lax.rem(y + dy, NY), c)

    def remote(src, dst, send, recv, device):
        return pltpu.make_async_remote_copy(
            src_ref=src,
            dst_ref=dst,
            send_sem=send,
            recv_sem=recv,
            device_id=device,
            device_id_type=MESH,
        )

    others = [(dx, dc) for dx in range(NX) for dc in range(2) if (dx, dc) != (0, 0)]

    loads = [
        pltpu.make_async_copy(
            hbm.at[pl.ds(ch * step, step)], kv_ref.at[0, ch, c, x, kv], load_sem.at[kv, ch]
        )
        for ch in range(NCH)
        for kv, hbm in enumerate((k_hbm, v_hbm))
    ]
    q_load = pltpu.make_async_copy(q_hbm, q_ref, load_sem.at[2, 0])
    for load in loads:
        load.start()
    q_load.start()
    zpart_ref[...] = jnp.zeros_like(zpart_ref)

    barrier = pltpu.get_barrier_semaphore()
    opposite = at(1 - z_hi, z_lo, x, y, c)
    greeted = [near(dx, dc) for dx, dc in others]
    greeted += [along_y(dy) for dy in range(1, NY)]
    greeted += [opposite]
    for d in range(1, NZ):
        for e in range(2):
            greeted.append(at(lax.rem(z_hi + e, 2), lax.rem(z_lo + d, NZ), x, y, c))
    for device in greeted:
        pl.semaphore_signal(barrier, inc=1, device_id=device, device_id_type=MESH)

    for load in loads:
        load.wait()
    for k in range(KVH):
        cols = pl.ds(k * HD, HD)
        key = kv_ref[0, :, c, x, 0, :, cols].reshape(rows, HD)
        value = kv_ref[0, :, c, x, 1, :, cols].reshape(rows, HD)
        partial_ref[pl.ds(k * 4, 4)] = lax.dot_general(
            sigma_map(key), value, TN, precision=HIGH, preferred_element_type=jnp.float32
        ).reshape(4, 32, HD)
    q_load.wait()
    scale = LOG2E / (HD**0.5)
    for k in range(KVH):
        for g in range(GROUP):
            h = k * GROUP + g
            top, low = halves(q_ref[:, pl.ds(h * HD, HD)] * scale)
            qs_ref[k, pl.ds(g * rows, rows), pl.ds(0, HD)] = top
            qs_ref[k, pl.ds(g * rows, rows), pl.ds(HD, HD)] = low
    m_ref[...] = jnp.full_like(m_ref, MASKED)
    l_ref[...] = jnp.zeros_like(l_ref)
    acc_ref[...] = jnp.zeros_like(acc_ref)

    pl.semaphore_wait(barrier, len(greeted))

    def across(ch):
        return remote(
            kv_ref.at[0, ch, c, x], kv_ref.at[1, ch, c, x], zs.at[ch], zr.at[ch], opposite
        )

    def spread(half, ch, dx):
        item = kv_ref.at[half, ch, c, x]
        return remote(
            item, item, xs.at[half, ch, dx - 1], xr.at[half, ch, dx - 1], near(dx, 0)
        )

    def share(half, ch, dx):
        item = kv_ref.at[half, ch, c, lax.rem(x + NX - dx, NX)]
        return remote(item, item, ss.at[half, ch, dx], sr.at[half, ch, dx], near(0, 1))

    nearest = (z_lo == 0) | (z_lo == NZ - 1)

    @pl.when((z_hi == 0) & nearest)
    def _():
        for ch in range(NCH):
            across(ch).start()

    def scatter(n):
        dx, dc = others[n]
        target = lax.rem(x + dx, NX) * 2 + lax.rem(c + dc, 2)
        return remote(
            partial_ref.at[target], parts_ref.at[j], ps.at[n], pr.at[n], near(dx, dc)
        )

    for n in range(len(others)):
        scatter(n).start()
    parts_ref[j] = partial_ref[j]

    def begin(half, ch):
        for dx in range(1, NX):
            spread(half, ch, dx).start()
        share(half, ch, 0).start()

    def pass_on(half, ch):
        for dx in range(1, NX):
            spread(half, ch, dx).wait_recv()
            share(half, ch, dx).start()

    def arrive(half, ch):
        for dx in range(NX):
            share(half, ch, dx).wait_recv()

    @pl.loop(0, NCH)
    def _(ch):
        begin(0, ch)

    for n in range(len(others)):
        scatter(n).wait_recv()
    shard_ref[...] = jnp.sum(parts_ref[...], axis=0).reshape(NY, 8, HD)

    def turn(dy):
        return remote(
            shard_ref.at[lax.rem(y + dy, NY)],
            ypart_ref.at[y],
            ys.at[dy - 1],
            yr.at[dy - 1],
            along_y(dy),
        )

    for dy in range(1, NY):
        turn(dy).start()
    ypart_ref[y] = shard_ref[y]
    for dy in range(1, NY):
        turn(dy).wait_recv()
    total_ref[...] = jnp.sum(ypart_ref[...], axis=0)

    def onward(d, e):
        return remote(
            total_ref,
            zpart_ref.at[d - 1, e],
            ts.at[d - 1, e],
            tr.at[d - 1, e],
            at(lax.rem(z_hi + e, 2), lax.rem(z_lo + d, NZ), x, y, c),
        )

    over = remote(ypart_ref, other_ref, fs, fr, opposite)
    over.start()
    for d in range(1, NZ):

        @pl.when(z_lo + d < NZ)
        def _(d=d):
            for e in range(2):
                onward(d, e).start()

    @pl.when((z_hi == 0) & jnp.logical_not(nearest))
    def _():
        for ch in range(NCH):
            across(ch).start()

    @pl.loop(0, NCH)
    def _(ch):
        pass_on(0, ch)

    qpos = j * rows + lax.rem(
        lax.broadcasted_iota(jnp.int32, (GROUP * rows, 2 * HD), 0), rows
    )
    slot = lax.broadcasted_iota(jnp.int32, (GROUP * rows, 2 * HD), 1)
    per = NX * step
    base_kpos = (
        lax.rem(lax.div(slot, step), NX) * 2 + lax.div(slot, per)
    ) * rows + lax.rem(slot, step)

    def attend(half, ch):
        for k in range(KVH):
            cols = pl.ds(k * HD, HD)
            key = kv_ref[half, ch, :, :, 0, :, cols].reshape(2 * NX * step, HD)
            value = kv_ref[half, ch, :, :, 1, :, cols].reshape(2 * NX * step, HD)
            k_top, k_low = halves(key)
            v_both = jnp.concatenate(halves(value), axis=1)
            q_both = qs_ref[k]
            scores = mm(q_both, jnp.concatenate((k_top, k_top), axis=1), NT)
            scores += mm(qs_ref[k, :, pl.ds(0, HD)], k_low, NT)
            if half == 0:
                scores = jnp.where(base_kpos + ch * step <= qpos, scores, MASKED)
            old = m_ref[k]
            new = jnp.maximum(old, jnp.max(scores, axis=1, keepdims=True))
            m_ref[k] = new
            decay = jnp.exp2(old - new)
            weights = jnp.exp2(scores - jnp.concatenate((new, new), axis=1))
            l_ref[k] = l_ref[k] * decay + weights[:, :HD] + weights[:, HD:]
            w_top, w_low = halves(weights)
            both = mm(w_top, v_both, NN) + mm(w_low, v_both, NN)
            acc_ref[k] = acc_ref[k] * decay + both[:, :HD] + both[:, HD:]

    def attend_near(start, stop):
        @pl.loop(start, stop)
        def _(ch):
            arrive(0, ch)
            attend(0, ch)

    def back(dy):
        return remote(
            stage_ref.at[lax.rem(y + dy, NY)],
            own_ref.at[y],
            ms.at[dy - 1],
            mr.at[dy - 1],
            along_y(dy),
        )

    def gather(n):
        dx, dc = others[n]
        return remote(own_ref, memory_ref.at[j], gs.at[n], gr.at[n], near(dx, dc))

    def carry():
        for d in range(1, NZ):

            @pl.when(z_lo >= d)
            def _(d=d):
                for e in range(2):
                    onward(d, e).wait_recv()

        over.wait_recv()
        carried = jnp.sum(zpart_ref[...], axis=(0, 1))
        for row in range(NY):
            stage_ref[row] = carried
            carried = carried + ypart_ref[row] + other_ref[row]
        for dy in range(1, NY):
            back(dy).start()
        own_ref[y] = stage_ref[y]

    def collect():
        for dy in range(1, NY):
            back(dy).wait_recv()
        for n in range(len(others)):
            gather(n).start()
        memory_ref[j] = own_ref[...]

    gates = 1.0 / (1.0 + jnp.exp(-gate_ref[...]))

    def retrieve():
        for n in range(len(others)):
            gather(n).wait_recv()
        for k in range(KVH):
            memory = memory_ref[pl.ds(k * 4, 4)].reshape(HD, HD)
            for g in range(GROUP):
                h = k * GROUP + g
                cols = pl.ds(h * HD, HD)
                got = lax.dot_general(
                    sigma_map(q_ref[:, cols]),
                    memory,
                    NN,
                    precision=HIGH,
                    preferred_element_type=jnp.float32,
                )
                rms = jnp.sqrt(jnp.mean(got * got, axis=1, keepdims=True) + 1e-6)
                gate = gates[:, h : h + 1]
                o_ref[:, cols] = (got / rms) * (gain_ref[h : h + 1, :] * gate)

    @pl.when(z_hi == 0)
    def _():
        attend_near(0, NCH)
        carry()
        collect()
        retrieve()

    @pl.when(z_hi == 1)
    def _():
        attend_near(0, NCH)
        for ch in range(NCH):
            across(ch).wait_recv()
            begin(1, ch)
        pass_on(1, 0)
        pass_on(1, 1)
        arrive(1, 0)
        attend(1, 0)
        carry()
        pass_on(1, 2)
        arrive(1, 1)
        attend(1, 1)
        collect()
        pass_on(1, 3)
        arrive(1, 2)
        attend(1, 2)
        retrieve()
        arrive(1, 3)
        attend(1, 3)

    @pl.when(z_hi == 1)
    def _():
        @pl.loop(0, NCH)
        def _(ch):
            for dx in range(1, NX):
                spread(1, ch, dx).wait_send()
            for dx in range(NX):
                share(1, ch, dx).wait_send()

    for k in range(KVH):
        for g in range(GROUP):
            h = k * GROUP + g
            cols = pl.ds(h * HD, HD)
            part = pl.ds(g * rows, rows)
            total = jnp.sum(l_ref[k, part], axis=1, keepdims=True)
            gate = gates[:, h : h + 1]
            o_ref[:, cols] += acc_ref[k, part] * ((1.0 - gate) / total)

    @pl.when(z_hi == 0)
    def _():
        for ch in range(NCH):
            across(ch).wait_send()

    @pl.loop(0, NCH)
    def _(ch):
        for dx in range(1, NX):
            spread(0, ch, dx).wait_send()
        for dx in range(NX):
            share(0, ch, dx).wait_send()

    for n in range(len(others)):
        scatter(n).wait_send()
        gather(n).wait_send()
    for dy in range(1, NY):
        turn(dy).wait_send()
        back(dy).wait_send()
    over.wait_send()
    for d in range(1, NZ):

        @pl.when(z_lo + d < NZ)
        def _(d=d):
            for e in range(2):
                onward(d, e).wait_send()


def on_device(queries, keys, values, gate_logit, memory_gain):
    rows = queries.shape[0]
    heads = KVH * GROUP
    f32 = jnp.float32
    sem = pltpu.SemaphoreType.DMA
    peers = 2 * NX - 1
    return pl.pallas_call(
        kernel,
        out_shape=jax.ShapeDtypeStruct((rows, heads * HD), f32),
        in_specs=[pl.BlockSpec(memory_space=pl.ANY)] * 3
        + [pl.BlockSpec(memory_space=pltpu.VMEM)] * 2,
        out_specs=pl.BlockSpec(memory_space=pltpu.VMEM),
        scratch_shapes=[
            pltpu.VMEM((rows, heads * HD), f32),
            pltpu.VMEM((2, NCH, 2, NX, 2, rows // NCH, KVH * HD), f32),
            pltpu.VMEM((KVH, GROUP * rows, 2 * HD), jnp.bfloat16),
            pltpu.VMEM((KVH, GROUP * rows, HD), f32),
            pltpu.VMEM((KVH, GROUP * rows, HD), f32),
            pltpu.VMEM((KVH, GROUP * rows, HD), f32),
            pltpu.VMEM((2 * NX, 32, HD), f32),
            pltpu.VMEM((2 * NX, 32, HD), f32),
            pltpu.VMEM((NY, 8, HD), f32),
            pltpu.VMEM((NY, 8, HD), f32),
            pltpu.VMEM((8, HD), f32),
            pltpu.VMEM((NZ - 1, 2, 8, HD), f32),
            pltpu.VMEM((NY, 8, HD), f32),
            pltpu.VMEM((NY, 8, HD), f32),
            pltpu.VMEM((NY, 8, HD), f32),
            pltpu.VMEM((2 * NX, NY, 8, HD), f32),
            sem((3, NCH)),
            sem((NCH,)),
            sem((NCH,)),
            sem((2, NCH, NX - 1)),
            sem((2, NCH, NX - 1)),
            sem((2, NCH, NX)),
            sem((2, NCH, NX)),
            sem((peers,)),
            sem((peers,)),
            sem((NY - 1,)),
            sem((NY - 1,)),
            sem((NZ - 1, 2)),
            sem((NZ - 1, 2)),
            sem,
            sem,
            sem((NY - 1,)),
            sem((NY - 1,)),
            sem((peers,)),
            sem((peers,)),
        ],
        compiler_params=pltpu.CompilerParams(collective_id=0, has_side_effects=True),
    )(
        queries,
        keys,
        values,
        gate_logit.reshape(1, heads),
        memory_gain.reshape(heads, HD),
    )


def solution(mesh):
    return jax.shard_map(
        on_device,
        mesh=mesh,
        in_specs=(
            P(("seg", "blk"), None),
            P(("seg", "blk"), None),
            P(("seg", "blk"), None),
            P(),
            P(),
        ),
        out_specs=P(("seg", "blk"), None),
        check_vma=False,
    )
```

```python
import jax
import jax.numpy as jnp
from jax import lax
from jax.experimental import pallas as pl
from jax.experimental.pallas import tpu as pltpu
from jax.sharding import PartitionSpec as P

KVH = 2
GROUP = 4
HD = 128
NX = 4
NY = 4
NZ = 8
NCH = 4
LOG2E = 1.4426950408889634
MASKED = -1e30
MESH = pl.DeviceIdType.MESH
HIGH = lax.Precision.HIGHEST
NT = (((1,), (1,)), ((), ()))
TN = (((0,), (0,)), ((), ()))
NN = (((1,), (0,)), ((), ()))


def sigma_map(x):
    return jnp.where(x > 0, x + 1.0, jnp.exp(jnp.minimum(x, 0.0)))


def halves(x):
    top = x.astype(jnp.bfloat16)
    return top, (x - top.astype(jnp.float32)).astype(jnp.bfloat16)


def mm(a, b, dims):
    return lax.dot_general(a, b, dims, preferred_element_type=jnp.float32)


def kernel(
    q_hbm,
    k_hbm,
    v_hbm,
    gate_ref,
    gain_ref,
    o_ref,
    q_ref,
    kv_ref,
    qs_ref,
    m_ref,
    l_ref,
    acc_ref,
    partial_ref,
    parts_ref,
    shard_ref,
    ypart_ref,
    total_ref,
    zpart_ref,
    other_ref,
    stage_ref,
    own_ref,
    memory_ref,
    load_sem,
    zs,
    zr,
    xs,
    xr,
    ss,
    sr,
    ps,
    pr,
    ys,
    yr,
    ts,
    tr,
    fs,
    fr,
    ms,
    mr,
    gs,
    gr,
):
    seg = lax.axis_index("seg")
    blk = lax.axis_index("blk")
    z_lo = lax.div(seg, NY)
    y = lax.rem(seg, NY)
    z_hi = lax.div(blk, 2 * NX)
    j = lax.rem(blk, 2 * NX)
    x = lax.div(j, 2)
    c = lax.rem(j, 2)
    rows = q_ref.shape[0]
    step = rows // NCH

    def at(zh, zl, xx, yy, cc):
        return {"seg": zl * NY + yy, "blk": zh * 2 * NX + xx * 2 + cc}

    def near(dx, dc):
        return at(z_hi, z_lo, lax.rem(x + dx, NX), y, lax.rem(c + dc, 2))

    def along_y(dy):
        return at(z_hi, z_lo, x, lax.rem(y + dy, NY), c)

    def remote(src, dst, send, recv, device):
        return pltpu.make_async_remote_copy(
            src_ref=src,
            dst_ref=dst,
            send_sem=send,
            recv_sem=recv,
            device_id=device,
            device_id_type=MESH,
        )

    others = [(dx, dc) for dx in range(NX) for dc in range(2) if (dx, dc) != (0, 0)]

    loads = [
        pltpu.make_async_copy(
            hbm.at[pl.ds(ch * step, step)], kv_ref.at[0, ch, c, x, kv], load_sem.at[kv, ch]
        )
        for ch in range(NCH)
        for kv, hbm in enumerate((k_hbm, v_hbm))
    ]
    q_load = pltpu.make_async_copy(q_hbm, q_ref, load_sem.at[2, 0])
    for load in loads:
        load.start()
    q_load.start()
    zpart_ref[...] = jnp.zeros_like(zpart_ref)

    barrier = pltpu.get_barrier_semaphore()
    opposite = at(1 - z_hi, z_lo, x, y, c)
    greeted = [near(dx, dc) for dx, dc in others]
    greeted += [along_y(dy) for dy in range(1, NY)]
    greeted += [opposite]
    for d in range(1, NZ):
        for e in range(2):
            greeted.append(at(lax.rem(z_hi + e, 2), lax.rem(z_lo + d, NZ), x, y, c))
    for device in greeted:
        pl.semaphore_signal(barrier, inc=1, device_id=device, device_id_type=MESH)

    for load in loads:
        load.wait()
    for k in range(KVH):
        cols = pl.ds(k * HD, HD)
        key = kv_ref[0, :, c, x, 0, :, cols].reshape(rows, HD)
        value = kv_ref[0, :, c, x, 1, :, cols].reshape(rows, HD)
        partial_ref[pl.ds(k * 4, 4)] = lax.dot_general(
            sigma_map(key), value, TN, precision=HIGH, preferred_element_type=jnp.float32
        ).reshape(4, 32, HD)
    q_load.wait()
    scale = LOG2E / (HD**0.5)
    for k in range(KVH):
        for g in range(GROUP):
            h = k * GROUP + g
            top, low = halves(q_ref[:, pl.ds(h * HD, HD)] * scale)
            qs_ref[k, pl.ds(g * rows, rows), pl.ds(0, HD)] = top
            qs_ref[k, pl.ds(g * rows, rows), pl.ds(HD, HD)] = low
    m_ref[...] = jnp.full_like(m_ref, MASKED)
    l_ref[...] = jnp.zeros_like(l_ref)
    acc_ref[...] = jnp.zeros_like(acc_ref)

    pl.semaphore_wait(barrier, len(greeted))

    def across(ch):
        return remote(
            kv_ref.at[0, ch, c, x], kv_ref.at[1, ch, c, x], zs.at[ch], zr.at[ch], opposite
        )

    def spread(half, ch, dx):
        item = kv_ref.at[half, ch, c, x]
        return remote(
            item, item, xs.at[half, ch, dx - 1], xr.at[half, ch, dx - 1], near(dx, 0)
        )

    def share(half, ch, dx):
        item = kv_ref.at[half, ch, c, lax.rem(x + NX - dx, NX)]
        return remote(item, item, ss.at[half, ch, dx], sr.at[half, ch, dx], near(0, 1))

    @pl.when(z_hi == 0)
    def _():
        for ch in range(NCH):
            across(ch).start()

    def scatter(n):
        dx, dc = others[n]
        target = lax.rem(x + dx, NX) * 2 + lax.rem(c + dc, 2)
        return remote(
            partial_ref.at[target], parts_ref.at[j], ps.at[n], pr.at[n], near(dx, dc)
        )

    for n in range(len(others)):
        scatter(n).start()
    parts_ref[j] = partial_ref[j]

    def begin(half, ch):
        for dx in range(1, NX):
            spread(half, ch, dx).start()
        share(half, ch, 0).start()

    def pass_on(half, ch):
        for dx in range(1, NX):
            spread(half, ch, dx).wait_recv()
            share(half, ch, dx).start()

    def arrive(half, ch):
        for dx in range(NX):
            share(half, ch, dx).wait_recv()

    @pl.loop(0, NCH)
    def _(ch):
        begin(0, ch)

    for n in range(len(others)):
        scatter(n).wait_recv()
    shard_ref[...] = jnp.sum(parts_ref[...], axis=0).reshape(NY, 8, HD)

    def turn(dy):
        return remote(
            shard_ref.at[lax.rem(y + dy, NY)],
            ypart_ref.at[y],
            ys.at[dy - 1],
            yr.at[dy - 1],
            along_y(dy),
        )

    for dy in range(1, NY):
        turn(dy).start()
    ypart_ref[y] = shard_ref[y]
    for dy in range(1, NY):
        turn(dy).wait_recv()
    total_ref[...] = jnp.sum(ypart_ref[...], axis=0)

    def onward(d, e):
        return remote(
            total_ref,
            zpart_ref.at[d - 1, e],
            ts.at[d - 1, e],
            tr.at[d - 1, e],
            at(lax.rem(z_hi + e, 2), lax.rem(z_lo + d, NZ), x, y, c),
        )

    over = remote(ypart_ref, other_ref, fs, fr, opposite)
    over.start()
    for d in range(1, NZ):

        @pl.when(z_lo + d < NZ)
        def _(d=d):
            for e in range(2):
                onward(d, e).start()

    @pl.loop(0, NCH)
    def _(ch):
        pass_on(0, ch)

    qpos = j * rows + lax.rem(
        lax.broadcasted_iota(jnp.int32, (GROUP * rows, 2 * HD), 0), rows
    )
    slot = lax.broadcasted_iota(jnp.int32, (GROUP * rows, 2 * HD), 1)
    per = NX * step
    base_kpos = (
        lax.rem(lax.div(slot, step), NX) * 2 + lax.div(slot, per)
    ) * rows + lax.rem(slot, step)

    def attend(half, ch):
        for k in range(KVH):
            cols = pl.ds(k * HD, HD)
            key = kv_ref[half, ch, :, :, 0, :, cols].reshape(2 * NX * step, HD)
            value = kv_ref[half, ch, :, :, 1, :, cols].reshape(2 * NX * step, HD)
            k_top, k_low = halves(key)
            v_both = jnp.concatenate(halves(value), axis=1)
            q_both = qs_ref[k]
            scores = mm(q_both, jnp.concatenate((k_top, k_top), axis=1), NT)
            scores += mm(qs_ref[k, :, pl.ds(0, HD)], k_low, NT)
            if half == 0:
                scores = jnp.where(base_kpos + ch * step <= qpos, scores, MASKED)
            old = m_ref[k]
            new = jnp.maximum(old, jnp.max(scores, axis=1, keepdims=True))
            m_ref[k] = new
            decay = jnp.exp2(old - new)
            weights = jnp.exp2(scores - jnp.concatenate((new, new), axis=1))
            l_ref[k] = l_ref[k] * decay + weights[:, :HD] + weights[:, HD:]
            w_top, w_low = halves(weights)
            both = mm(w_top, v_both, NN) + mm(w_low, v_both, NN)
            acc_ref[k] = acc_ref[k] * decay + both[:, :HD] + both[:, HD:]

    def attend_near(start, stop):
        @pl.loop(start, stop)
        def _(ch):
            arrive(0, ch)
            attend(0, ch)

    def back(dy):
        return remote(
            stage_ref.at[lax.rem(y + dy, NY)],
            own_ref.at[y],
            ms.at[dy - 1],
            mr.at[dy - 1],
            along_y(dy),
        )

    def gather(n):
        dx, dc = others[n]
        return remote(own_ref, memory_ref.at[j], gs.at[n], gr.at[n], near(dx, dc))

    def carry():
        for d in range(1, NZ):

            @pl.when(z_lo >= d)
            def _(d=d):
                for e in range(2):
                    onward(d, e).wait_recv()

        over.wait_recv()
        carried = jnp.sum(zpart_ref[...], axis=(0, 1))
        for row in range(NY):
            stage_ref[row] = carried
            carried = carried + ypart_ref[row] + other_ref[row]
        for dy in range(1, NY):
            back(dy).start()
        own_ref[y] = stage_ref[y]

    def collect():
        for dy in range(1, NY):
            back(dy).wait_recv()
        for n in range(len(others)):
            gather(n).start()
        memory_ref[j] = own_ref[...]

    gates = 1.0 / (1.0 + jnp.exp(-gate_ref[...]))

    def retrieve():
        for n in range(len(others)):
            gather(n).wait_recv()
        for k in range(KVH):
            memory = memory_ref[pl.ds(k * 4, 4)].reshape(HD, HD)
            for g in range(GROUP):
                h = k * GROUP + g
                cols = pl.ds(h * HD, HD)
                got = lax.dot_general(
                    sigma_map(q_ref[:, cols]),
                    memory,
                    NN,
                    precision=HIGH,
                    preferred_element_type=jnp.float32,
                )
                rms = jnp.sqrt(jnp.mean(got * got, axis=1, keepdims=True) + 1e-6)
                gate = gates[:, h : h + 1]
                o_ref[:, cols] = (got / rms) * (gain_ref[h : h + 1, :] * gate)

    @pl.when(z_hi == 0)
    def _():
        attend_near(0, NCH)
        carry()
        collect()
        retrieve()

    @pl.when(z_hi == 1)
    def _():
        attend_near(0, NCH)
        for ch in range(NCH):
            across(ch).wait_recv()
            begin(1, ch)
        pass_on(1, 0)
        pass_on(1, 1)
        carry()
        arrive(1, 0)
        attend(1, 0)
        pass_on(1, 2)
        collect()
        arrive(1, 1)
        attend(1, 1)
        pass_on(1, 3)
        arrive(1, 2)
        attend(1, 2)
        retrieve()
        arrive(1, 3)
        attend(1, 3)

    @pl.when(z_hi == 1)
    def _():
        @pl.loop(0, NCH)
        def _(ch):
            for dx in range(1, NX):
                spread(1, ch, dx).wait_send()
            for dx in range(NX):
                share(1, ch, dx).wait_send()

    for k in range(KVH):
        for g in range(GROUP):
            h = k * GROUP + g
            cols = pl.ds(h * HD, HD)
            part = pl.ds(g * rows, rows)
            total = jnp.sum(l_ref[k, part], axis=1, keepdims=True)
            gate = gates[:, h : h + 1]
            o_ref[:, cols] += acc_ref[k, part] * ((1.0 - gate) / total)

    @pl.when(z_hi == 0)
    def _():
        for ch in range(NCH):
            across(ch).wait_send()

    @pl.loop(0, NCH)
    def _(ch):
        for dx in range(1, NX):
            spread(0, ch, dx).wait_send()
        for dx in range(NX):
            share(0, ch, dx).wait_send()

    for n in range(len(others)):
        scatter(n).wait_send()
        gather(n).wait_send()
    for dy in range(1, NY):
        turn(dy).wait_send()
        back(dy).wait_send()
    over.wait_send()
    for d in range(1, NZ):

        @pl.when(z_lo + d < NZ)
        def _(d=d):
            for e in range(2):
                onward(d, e).wait_send()


def on_device(queries, keys, values, gate_logit, memory_gain):
    rows = queries.shape[0]
    heads = KVH * GROUP
    f32 = jnp.float32
    sem = pltpu.SemaphoreType.DMA
    peers = 2 * NX - 1
    return pl.pallas_call(
        kernel,
        out_shape=jax.ShapeDtypeStruct((rows, heads * HD), f32),
        in_specs=[pl.BlockSpec(memory_space=pl.ANY)] * 3
        + [pl.BlockSpec(memory_space=pltpu.VMEM)] * 2,
        out_specs=pl.BlockSpec(memory_space=pltpu.VMEM),
        scratch_shapes=[
            pltpu.VMEM((rows, heads * HD), f32),
            pltpu.VMEM((2, NCH, 2, NX, 2, rows // NCH, KVH * HD), f32),
            pltpu.VMEM((KVH, GROUP * rows, 2 * HD), jnp.bfloat16),
            pltpu.VMEM((KVH, GROUP * rows, HD), f32),
            pltpu.VMEM((KVH, GROUP * rows, HD), f32),
            pltpu.VMEM((KVH, GROUP * rows, HD), f32),
            pltpu.VMEM((2 * NX, 32, HD), f32),
            pltpu.VMEM((2 * NX, 32, HD), f32),
            pltpu.VMEM((NY, 8, HD), f32),
            pltpu.VMEM((NY, 8, HD), f32),
            pltpu.VMEM((8, HD), f32),
            pltpu.VMEM((NZ - 1, 2, 8, HD), f32),
            pltpu.VMEM((NY, 8, HD), f32),
            pltpu.VMEM((NY, 8, HD), f32),
            pltpu.VMEM((NY, 8, HD), f32),
            pltpu.VMEM((2 * NX, NY, 8, HD), f32),
            sem((3, NCH)),
            sem((NCH,)),
            sem((NCH,)),
            sem((2, NCH, NX - 1)),
            sem((2, NCH, NX - 1)),
            sem((2, NCH, NX)),
            sem((2, NCH, NX)),
            sem((peers,)),
            sem((peers,)),
            sem((NY - 1,)),
            sem((NY - 1,)),
            sem((NZ - 1, 2)),
            sem((NZ - 1, 2)),
            sem,
            sem,
            sem((NY - 1,)),
            sem((NY - 1,)),
            sem((peers,)),
            sem((peers,)),
        ],
        compiler_params=pltpu.CompilerParams(collective_id=0, has_side_effects=True),
    )(
        queries,
        keys,
        values,
        gate_logit.reshape(1, heads),
        memory_gain.reshape(heads, HD),
    )


def solution(mesh):
    return jax.shard_map(
        on_device,
        mesh=mesh,
        in_specs=(
            P(("seg", "blk"), None),
            P(("seg", "blk"), None),
            P(("seg", "blk"), None),
            P(),
            P(),
        ),
        out_specs=P(("seg", "blk"), None),
        check_vma=False,
    )
```

```python
import jax
import jax.numpy as jnp
from jax import lax
from jax.experimental import pallas as pl
from jax.experimental.pallas import tpu as pltpu
from jax.sharding import PartitionSpec as P

KVH = 2
GROUP = 4
HD = 128
NX = 4
NY = 4
NZ = 8
NCH = 4
LOG2E = 1.4426950408889634
MASKED = -1e30
MESH = pl.DeviceIdType.MESH
HIGH = lax.Precision.HIGHEST
NT = (((1,), (1,)), ((), ()))
TN = (((0,), (0,)), ((), ()))
NN = (((1,), (0,)), ((), ()))


def sigma_map(x):
    return jnp.where(x > 0, x + 1.0, jnp.exp(jnp.minimum(x, 0.0)))


def halves(x):
    top = x.astype(jnp.bfloat16)
    return top, (x - top.astype(jnp.float32)).astype(jnp.bfloat16)


def mm(a, b, dims):
    return lax.dot_general(a, b, dims, preferred_element_type=jnp.float32)


def kernel(
    q_hbm,
    k_hbm,
    v_hbm,
    gate_ref,
    gain_ref,
    o_ref,
    q_ref,
    kv_ref,
    qs_ref,
    m_ref,
    l_ref,
    acc_ref,
    partial_ref,
    parts_ref,
    shard_ref,
    ypart_ref,
    total_ref,
    zpart_ref,
    other_ref,
    stage_ref,
    own_ref,
    memory_ref,
    load_sem,
    zs,
    zr,
    xs,
    xr,
    ss,
    sr,
    ps,
    pr,
    ys,
    yr,
    ts,
    tr,
    fs,
    fr,
    ms,
    mr,
    gs,
    gr,
):
    seg = lax.axis_index("seg")
    blk = lax.axis_index("blk")
    z_lo = lax.div(seg, NY)
    y = lax.rem(seg, NY)
    z_hi = lax.div(blk, 2 * NX)
    j = lax.rem(blk, 2 * NX)
    x = lax.div(j, 2)
    c = lax.rem(j, 2)
    rows = q_ref.shape[0]
    step = rows // NCH

    def at(zh, zl, xx, yy, cc):
        return {"seg": zl * NY + yy, "blk": zh * 2 * NX + xx * 2 + cc}

    def near(dx, dc):
        return at(z_hi, z_lo, lax.rem(x + dx, NX), y, lax.rem(c + dc, 2))

    def along_y(dy):
        return at(z_hi, z_lo, x, lax.rem(y + dy, NY), c)

    def remote(src, dst, send, recv, device):
        return pltpu.make_async_remote_copy(
            src_ref=src,
            dst_ref=dst,
            send_sem=send,
            recv_sem=recv,
            device_id=device,
            device_id_type=MESH,
        )

    others = [(dx, dc) for dx in range(NX) for dc in range(2) if (dx, dc) != (0, 0)]

    loads = [
        pltpu.make_async_copy(
            hbm.at[pl.ds(ch * step, step)], kv_ref.at[0, ch, c, x, kv], load_sem.at[kv, ch]
        )
        for ch in range(NCH)
        for kv, hbm in enumerate((k_hbm, v_hbm))
    ]
    q_load = pltpu.make_async_copy(q_hbm, q_ref, load_sem.at[2, 0])
    for load in loads:
        load.start()
    q_load.start()
    zpart_ref[...] = jnp.zeros_like(zpart_ref)

    barrier = pltpu.get_barrier_semaphore()
    opposite = at(1 - z_hi, z_lo, x, y, c)
    greeted = [near(dx, dc) for dx, dc in others]
    greeted += [along_y(dy) for dy in range(1, NY)]
    greeted += [opposite]
    for d in range(1, NZ):
        for e in range(2):
            greeted.append(at(lax.rem(z_hi + e, 2), lax.rem(z_lo + d, NZ), x, y, c))
    for device in greeted:
        pl.semaphore_signal(barrier, inc=1, device_id=device, device_id_type=MESH)

    for load in loads:
        load.wait()
    for k in range(KVH):
        cols = pl.ds(k * HD, HD)
        key = kv_ref[0, :, c, x, 0, :, cols].reshape(rows, HD)
        value = kv_ref[0, :, c, x, 1, :, cols].reshape(rows, HD)
        partial_ref[pl.ds(k * 4, 4)] = lax.dot_general(
            sigma_map(key), value, TN, precision=HIGH, preferred_element_type=jnp.float32
        ).reshape(4, 32, HD)
    q_load.wait()
    scale = LOG2E / (HD**0.5)
    for k in range(KVH):
        for g in range(GROUP):
            h = k * GROUP + g
            top, low = halves(q_ref[:, pl.ds(h * HD, HD)] * scale)
            qs_ref[k, pl.ds(g * rows, rows), pl.ds(0, HD)] = top
            qs_ref[k, pl.ds(g * rows, rows), pl.ds(HD, HD)] = low
    m_ref[...] = jnp.full_like(m_ref, MASKED)
    l_ref[...] = jnp.zeros_like(l_ref)
    acc_ref[...] = jnp.zeros_like(acc_ref)

    pl.semaphore_wait(barrier, len(greeted))

    def across(ch):
        return remote(
            kv_ref.at[0, ch, c, x], kv_ref.at[1, ch, c, x], zs.at[ch], zr.at[ch], opposite
        )

    def spread(half, ch, dx):
        item = kv_ref.at[half, ch, c, x]
        return remote(
            item, item, xs.at[half, ch, dx - 1], xr.at[half, ch, dx - 1], near(dx, 0)
        )

    def share(half, ch, dx):
        item = kv_ref.at[half, ch, c, lax.rem(x + NX - dx, NX)]
        return remote(item, item, ss.at[half, ch, dx], sr.at[half, ch, dx], near(0, 1))

    @pl.when(z_hi == 0)
    def _():
        for ch in range(NCH):
            across(ch).start()

    def scatter(n):
        dx, dc = others[n]
        target = lax.rem(x + dx, NX) * 2 + lax.rem(c + dc, 2)
        return remote(
            partial_ref.at[target], parts_ref.at[j], ps.at[n], pr.at[n], near(dx, dc)
        )

    for n in range(len(others)):
        scatter(n).start()
    parts_ref[j] = partial_ref[j]

    def begin(half, ch):
        for dx in (1, 3, 2):
            spread(half, ch, dx).start()
        share(half, ch, 0).start()

    def pass_on(half, ch):
        for dx in (1, 3, 2):
            spread(half, ch, dx).wait_recv()
            share(half, ch, dx).start()

    def arrive(half, ch):
        for dx in range(NX):
            share(half, ch, dx).wait_recv()

    @pl.loop(0, NCH)
    def _(ch):
        begin(0, ch)

    for n in range(len(others)):
        scatter(n).wait_recv()
    shard_ref[...] = jnp.sum(parts_ref[...], axis=0).reshape(NY, 8, HD)

    def turn(dy):
        return remote(
            shard_ref.at[lax.rem(y + dy, NY)],
            ypart_ref.at[y],
            ys.at[dy - 1],
            yr.at[dy - 1],
            along_y(dy),
        )

    for dy in range(1, NY):
        turn(dy).start()
    ypart_ref[y] = shard_ref[y]
    for dy in range(1, NY):
        turn(dy).wait_recv()
    total_ref[...] = jnp.sum(ypart_ref[...], axis=0)

    def onward(d, e):
        return remote(
            total_ref,
            zpart_ref.at[d - 1, e],
            ts.at[d - 1, e],
            tr.at[d - 1, e],
            at(lax.rem(z_hi + e, 2), lax.rem(z_lo + d, NZ), x, y, c),
        )

    over = remote(ypart_ref, other_ref, fs, fr, opposite)
    over.start()
    for d in range(1, NZ):

        @pl.when(z_lo + d < NZ)
        def _(d=d):
            for e in range(2):
                onward(d, e).start()

    @pl.loop(0, NCH)
    def _(ch):
        pass_on(0, ch)

    qpos = j * rows + lax.rem(
        lax.broadcasted_iota(jnp.int32, (GROUP * rows, 2 * HD), 0), rows
    )
    slot = lax.broadcasted_iota(jnp.int32, (GROUP * rows, 2 * HD), 1)
    per = NX * step
    base_kpos = (
        lax.rem(lax.div(slot, step), NX) * 2 + lax.div(slot, per)
    ) * rows + lax.rem(slot, step)

    def attend(half, ch):
        for k in range(KVH):
            cols = pl.ds(k * HD, HD)
            key = kv_ref[half, ch, :, :, 0, :, cols].reshape(2 * NX * step, HD)
            value = kv_ref[half, ch, :, :, 1, :, cols].reshape(2 * NX * step, HD)
            k_top, k_low = halves(key)
            v_both = jnp.concatenate(halves(value), axis=1)
            q_both = qs_ref[k]
            scores = mm(q_both, jnp.concatenate((k_top, k_top), axis=1), NT)
            scores += mm(qs_ref[k, :, pl.ds(0, HD)], k_low, NT)
            if half == 0:
                scores = jnp.where(base_kpos + ch * step <= qpos, scores, MASKED)
            old = m_ref[k]
            new = jnp.maximum(old, jnp.max(scores, axis=1, keepdims=True))
            m_ref[k] = new
            decay = jnp.exp2(old - new)
            weights = jnp.exp2(scores - jnp.concatenate((new, new), axis=1))
            l_ref[k] = l_ref[k] * decay + weights[:, :HD] + weights[:, HD:]
            w_top, w_low = halves(weights)
            both = mm(w_top, v_both, NN) + mm(w_low, v_both, NN)
            acc_ref[k] = acc_ref[k] * decay + both[:, :HD] + both[:, HD:]

    def attend_near(start, stop):
        @pl.loop(start, stop)
        def _(ch):
            arrive(0, ch)
            attend(0, ch)

    def back(dy):
        return remote(
            stage_ref.at[lax.rem(y + dy, NY)],
            own_ref.at[y],
            ms.at[dy - 1],
            mr.at[dy - 1],
            along_y(dy),
        )

    def gather(n):
        dx, dc = others[n]
        return remote(own_ref, memory_ref.at[j], gs.at[n], gr.at[n], near(dx, dc))

    def carry():
        for d in range(1, NZ):

            @pl.when(z_lo >= d)
            def _(d=d):
                for e in range(2):
                    onward(d, e).wait_recv()

        over.wait_recv()
        carried = jnp.sum(zpart_ref[...], axis=(0, 1))
        for row in range(NY):
            stage_ref[row] = carried
            carried = carried + ypart_ref[row] + other_ref[row]
        for dy in range(1, NY):
            back(dy).start()
        own_ref[y] = stage_ref[y]

    def collect():
        for dy in range(1, NY):
            back(dy).wait_recv()
        for n in range(len(others)):
            gather(n).start()
        memory_ref[j] = own_ref[...]

    gates = 1.0 / (1.0 + jnp.exp(-gate_ref[...]))

    def retrieve():
        for n in range(len(others)):
            gather(n).wait_recv()
        for k in range(KVH):
            memory = memory_ref[pl.ds(k * 4, 4)].reshape(HD, HD)
            for g in range(GROUP):
                h = k * GROUP + g
                cols = pl.ds(h * HD, HD)
                got = lax.dot_general(
                    sigma_map(q_ref[:, cols]),
                    memory,
                    NN,
                    precision=HIGH,
                    preferred_element_type=jnp.float32,
                )
                rms = jnp.sqrt(jnp.mean(got * got, axis=1, keepdims=True) + 1e-6)
                gate = gates[:, h : h + 1]
                o_ref[:, cols] = (got / rms) * (gain_ref[h : h + 1, :] * gate)

    @pl.when(z_hi == 0)
    def _():
        attend_near(0, NCH)
        carry()
        collect()
        retrieve()

    @pl.when(z_hi == 1)
    def _():
        attend_near(0, NCH)
        for ch in range(NCH):
            across(ch).wait_recv()
            begin(1, ch)
        pass_on(1, 0)
        pass_on(1, 1)
        carry()
        pass_on(1, 2)
        arrive(1, 0)
        attend(1, 0)
        collect()
        pass_on(1, 3)
        arrive(1, 1)
        attend(1, 1)
        arrive(1, 2)
        attend(1, 2)
        retrieve()
        arrive(1, 3)
        attend(1, 3)

    @pl.when(z_hi == 1)
    def _():
        @pl.loop(0, NCH)
        def _(ch):
            for dx in range(1, NX):
                spread(1, ch, dx).wait_send()
            for dx in range(NX):
                share(1, ch, dx).wait_send()

    for k in range(KVH):
        for g in range(GROUP):
            h = k * GROUP + g
            cols = pl.ds(h * HD, HD)
            part = pl.ds(g * rows, rows)
            total = jnp.sum(l_ref[k, part], axis=1, keepdims=True)
            gate = gates[:, h : h + 1]
            o_ref[:, cols] += acc_ref[k, part] * ((1.0 - gate) / total)

    @pl.when(z_hi == 0)
    def _():
        for ch in range(NCH):
            across(ch).wait_send()

    @pl.loop(0, NCH)
    def _(ch):
        for dx in range(1, NX):
            spread(0, ch, dx).wait_send()
        for dx in range(NX):
            share(0, ch, dx).wait_send()

    for n in range(len(others)):
        scatter(n).wait_send()
        gather(n).wait_send()
    for dy in range(1, NY):
        turn(dy).wait_send()
        back(dy).wait_send()
    over.wait_send()
    for d in range(1, NZ):

        @pl.when(z_lo + d < NZ)
        def _(d=d):
            for e in range(2):
                onward(d, e).wait_send()


def on_device(queries, keys, values, gate_logit, memory_gain):
    rows = queries.shape[0]
    heads = KVH * GROUP
    f32 = jnp.float32
    sem = pltpu.SemaphoreType.DMA
    peers = 2 * NX - 1
    return pl.pallas_call(
        kernel,
        out_shape=jax.ShapeDtypeStruct((rows, heads * HD), f32),
        in_specs=[pl.BlockSpec(memory_space=pl.ANY)] * 3
        + [pl.BlockSpec(memory_space=pltpu.VMEM)] * 2,
        out_specs=pl.BlockSpec(memory_space=pltpu.VMEM),
        scratch_shapes=[
            pltpu.VMEM((rows, heads * HD), f32),
            pltpu.VMEM((2, NCH, 2, NX, 2, rows // NCH, KVH * HD), f32),
            pltpu.VMEM((KVH, GROUP * rows, 2 * HD), jnp.bfloat16),
            pltpu.VMEM((KVH, GROUP * rows, HD), f32),
            pltpu.VMEM((KVH, GROUP * rows, HD), f32),
            pltpu.VMEM((KVH, GROUP * rows, HD), f32),
            pltpu.VMEM((2 * NX, 32, HD), f32),
            pltpu.VMEM((2 * NX, 32, HD), f32),
            pltpu.VMEM((NY, 8, HD), f32),
            pltpu.VMEM((NY, 8, HD), f32),
            pltpu.VMEM((8, HD), f32),
            pltpu.VMEM((NZ - 1, 2, 8, HD), f32),
            pltpu.VMEM((NY, 8, HD), f32),
            pltpu.VMEM((NY, 8, HD), f32),
            pltpu.VMEM((NY, 8, HD), f32),
            pltpu.VMEM((2 * NX, NY, 8, HD), f32),
            sem((3, NCH)),
            sem((NCH,)),
            sem((NCH,)),
            sem((2, NCH, NX - 1)),
            sem((2, NCH, NX - 1)),
            sem((2, NCH, NX)),
            sem((2, NCH, NX)),
            sem((peers,)),
            sem((peers,)),
            sem((NY - 1,)),
            sem((NY - 1,)),
            sem((NZ - 1, 2)),
            sem((NZ - 1, 2)),
            sem,
            sem,
            sem((NY - 1,)),
            sem((NY - 1,)),
            sem((peers,)),
            sem((peers,)),
        ],
        compiler_params=pltpu.CompilerParams(collective_id=0, has_side_effects=True),
    )(
        queries,
        keys,
        values,
        gate_logit.reshape(1, heads),
        memory_gain.reshape(heads, HD),
    )


def solution(mesh):
    return jax.shard_map(
        on_device,
        mesh=mesh,
        in_specs=(
            P(("seg", "blk"), None),
            P(("seg", "blk"), None),
            P(("seg", "blk"), None),
            P(),
            P(),
        ),
        out_specs=P(("seg", "blk"), None),
        check_vma=False,
    )
```
